256 devices in a mesh: tm: 8 (over z_hi, y), space: 32 (over z_lo, x, core).
Axes of the slice: x: 4, y: 4, z: 8 (z_hi: 2, z_lo: 4; z = z_hi * 4 + z_lo), core: 2. Of those that a mesh axis runs over, the one named last changes fastest.
Arguments:
- member_average: float32 [128, 2880, 640], P('tm', 'space'), may hold values from -6 to 6
- member_spread_squared: float32 [128, 2880, 640], P('tm', 'space'), may hold values from 0.1 to 4
- measured_truth: float32 [128, 2880, 640], P('tm', 'space'), may hold values from -8 to 8
- coefficients: float32 [4, 2880, 640], P(None, 'space'), may hold values from -1 to 1
Outputs:
- updated: float32 [4, 2880, 640], P(None, 'space')
The draws below stay inside these ranges and needn't reach their ends.
All inputs are finite; a program needn't handle non-finite values.
Results may differ from the reference program's by a relative error of at most 0.00002.
Values sent between devices are 32-bit elements; how exact they have to be, the bound alone decides.
No kernel may reach another device: no remote copies, remote signals or barrier semaphores. Data moves between devices by JAX's collectives and lax.ppermute only.
A program may use at most 64 MiB of HBM per device.

```python
import math
import jax
import jax.numpy as jnp
from jax import lax

PARALLEL_LINES = 640
ITERS = 2
OUTLOOK_DATES = 128
MERIDIAN_NUMBER = 2880


def level_of(own_key, shape, shards, low, top_value):
    factor_of, own = 1.0, jax.random.fold_in(own_key, 6)
    for axis_at, blocks in shards:
        draws = jnp.exp(jax.random.uniform(jax.random.fold_in(own, axis_at), (blocks,), jnp.float32, low / len(shards), top_value / len(shards)))
        factor_of = factor_of * jnp.repeat(draws, shape[axis_at] // blocks).reshape([-1 if axis == axis_at else 1 for axis in range(len(shape))])
    return factor_of


def gaussian(rng, dims, deviation, most, shards=(), kind=jnp.bfloat16):
    result = deviation * jax.random.normal(rng, dims, jnp.float32)
    if shards:
        result = result * level_of(rng, dims, shards, -0.22, 0.18)
    return jnp.clip(result, -most, most).astype(kind)


def setup_inputs(seed: int = 0) -> dict:
    arg_keys = jax.random.split(jax.random.key(seed), 5)
    member_average = gaussian(arg_keys[0], (OUTLOOK_DATES, MERIDIAN_NUMBER, PARALLEL_LINES), 1.0, 6.0, ((0, 8), (1, 32)), jnp.float32)
    member_spread_squared = jnp.clip(jnp.exp(math.log(4.0) - 3.6888794 * jax.random.uniform(arg_keys[1], (OUTLOOK_DATES, MERIDIAN_NUMBER, PARALLEL_LINES), jnp.float32) ** level_of(arg_keys[1], (OUTLOOK_DATES, MERIDIAN_NUMBER, PARALLEL_LINES), ((0, 8), (1, 32)), -0.2, 0.2)), 0.1, 4.0)
    measured_truth = gaussian(arg_keys[2], (OUTLOOK_DATES, MERIDIAN_NUMBER, PARALLEL_LINES), 1.5, 8.0, ((0, 8), (1, 32)), jnp.float32)
    coefficients = jnp.clip(jax.random.uniform(arg_keys[3], (4, MERIDIAN_NUMBER, PARALLEL_LINES), jnp.float32, -1.0, 1.0) * level_of(arg_keys[3], (4, MERIDIAN_NUMBER, PARALLEL_LINES), ((1, 32),), -0.4, 0.0), -1.0, 1.0)
    return {"member_average": member_average, "member_spread_squared": member_spread_squared, "measured_truth": measured_truth, "coefficients": coefficients}


descent_factor = 0.5
smooth_weight = 0.03

def graph_laplace(field):
    along_lon = jnp.roll(field, 1, axis=-2) + jnp.roll(field, -1, axis=-2) - 2.0 * field
    steps_lat = field[..., 1:] - field[..., :-1]
    zero_col = jnp.zeros(field.shape[:-1] + (1,), jnp.float32)
    along_lat = jnp.concatenate([steps_lat, zero_col], axis=-1) - jnp.concatenate([zero_col, steps_lat], axis=-1)
    return along_lon + along_lat

def daily_score_parts(calibration_coefficients_set, fmean, fvar, obs):
    base_exp = jnp.exp(calibration_coefficients_set[2])
    spread = jnp.sqrt(base_exp + calibration_coefficients_set[3] * calibration_coefficients_set[3] * fvar)
    center = calibration_coefficients_set[0] + calibration_coefficients_set[1] * fmean
    standard = (obs - center) / spread
    cumulative = 0.5 * (1.0 + jax.scipy.special.erf(standard * 0.7071067811865476))
    density = jnp.exp(-0.5 * standard * standard) * 0.3989422804014327
    dcenter = 1.0 - 2.0 * cumulative
    dvar = (2.0 * density - 0.5641895835477563) / (2.0 * spread)
    return jnp.stack([dcenter, dcenter * fmean, dvar * base_exp, dvar * 2.0 * calibration_coefficients_set[3] * fvar])

def reference(member_average, member_spread_squared, measured_truth, coefficients):
    calibration_coefficients_set = coefficients
    for step in range(ITERS):

        def accumulate_day(aggregate_loss, day):
            return (aggregate_loss + daily_score_parts(calibration_coefficients_set, day[0], day[1], day[2]), None)
        aggregate_loss, ignored_carry = lax.scan(accumulate_day, jnp.zeros(calibration_coefficients_set.shape, jnp.float32), (member_average, member_spread_squared, measured_truth))
        roughness_cost = smooth_weight * graph_laplace(graph_laplace(calibration_coefficients_set))
        calibration_coefficients_set = calibration_coefficients_set - descent_factor * (aggregate_loss / OUTLOOK_DATES + roughness_cost)
    return calibration_coefficients_set
```

```python
import jax
import jax.numpy as jnp
from jax import lax
from jax.sharding import PartitionSpec as P

ITERS = 2
STEP = 0.5
SMOOTH = 0.03
Y = 4


def pairs(count, partner):
    return [(i, partner(i)) for i in range(count)]


def swap_low(i):
    return i ^ 1


def swap_high(i):
    return i ^ 3


def swap_z(i):
    return i ^ Y


def exchange(block, partner):
    return lax.ppermute(block, "tm", pairs(lax.axis_size("tm"), partner))


def day_sums(theta, fmean, fvar, obs):
    base_exp = jnp.exp(theta[2])
    spread = jnp.sqrt(base_exp + theta[3] * theta[3] * fvar)
    center = theta[0] + theta[1] * fmean
    standard = (obs - center) / spread
    cumulative = 0.5 * (1.0 + jax.scipy.special.erf(standard * 0.7071067811865476))
    density = jnp.exp(-0.5 * standard * standard) * 0.3989422804014327
    dcenter = 1.0 - 2.0 * cumulative
    dvar = (2.0 * density - 0.5641895835477563) / (2.0 * spread)
    return (
        jnp.sum(dcenter, axis=0),
        jnp.sum(dcenter * fmean, axis=0),
        jnp.sum(dvar * base_exp, axis=0),
        jnp.sum(dvar * 2.0 * theta[3] * fvar, axis=0),
    )


def laplace(extended):
    middle = extended[1:-1]
    along_lon = extended[2:] + extended[:-2] - 2.0 * middle
    steps = middle[:, 1:] - middle[:, :-1]
    zero = jnp.zeros((middle.shape[0], 1), jnp.float32)
    return along_lon + (
        jnp.concatenate([steps, zero], axis=1) - jnp.concatenate([zero, steps], axis=1)
    )


def smoothed(field):
    count = lax.axis_size("space")
    low = lax.ppermute(field[-2:], "space", pairs(count, lambda i: (i + 1) % count))
    high = lax.ppermute(field[:2], "space", pairs(count, lambda i: (i - 1) % count))
    extended = jnp.concatenate([low, field, high], axis=0)
    return field - (STEP * SMOOTH) * laplace(laplace(extended))


def on_device(fmean, fvar, obs, theta):
    days = fmean.shape[0] * lax.axis_size("tm")
    at_y = lax.axis_index("tm") % Y
    high = at_y // 2
    low = (at_y ^ high) % 2
    first_low, first_high = low == 0, high == 0
    mine = jnp.where(
        first_high, jnp.where(first_low, theta[0], theta[1]), jnp.where(first_low, theta[2], theta[3])
    )
    for _ in range(ITERS):
        base = smoothed(mine)
        s = day_sums(theta, fmean, fvar, obs)
        keep = [jnp.where(first_low, s[0], s[1]), jnp.where(first_low, s[2], s[3])]
        send = jnp.stack([jnp.where(first_low, s[1], s[0]), jnp.where(first_low, s[3], s[2])])
        got = exchange(send, swap_low)
        send = jnp.where(first_high, keep[1] + got[1], keep[0] + got[0])
        keep = jnp.where(first_high, keep[0] + got[0], keep[1] + got[1])
        total = keep + exchange(send, swap_high)
        total = total + exchange(total, swap_z)
        mine = base - (STEP / days) * total
        other = exchange(mine, swap_high)
        pair = jnp.stack([jnp.where(first_high, mine, other), jnp.where(first_high, other, mine)])
        across = exchange(pair, swap_low)
        theta = jnp.stack(
            [
                jnp.where(first_low, pair[0], across[0]),
                jnp.where(first_low, across[0], pair[0]),
                jnp.where(first_low, pair[1], across[1]),
                jnp.where(first_low, across[1], pair[1]),
            ]
        )
    return theta


def solution(mesh):
    days = P("tm", "space", None)
    fields = P(None, "space", None)
    return jax.shard_map(
        on_device,
        mesh=mesh,
        in_specs=(days, days, days, fields),
        out_specs=fields,
        check_vma=False,
    )
```

```python
import functools

import jax
import jax.numpy as jnp
from jax import lax
from jax.experimental import pallas as pl
from jax.experimental.pallas import tpu as pltpu
from jax.sharding import PartitionSpec as P


ITERS = 2
STEP = 0.5
SMOOTH = 0.03
Y = 4
ORDER = (2, 1, 3, 0)
GROUP = 4

BEND = 0.33
TAIL = (
    0.24258075161877687,
    0.4135445348314681,
    -0.19449665181676495,
    0.7602243169976308,
    -0.22185304956855628,
)
UNIT = (-TAIL[4]) ** 0.2
TAIL_UNIT = tuple(c / UNIT ** (i + 1) for i, c in enumerate(TAIL[:4]))
GAUGE = BEND / UNIT
POWER = -0.7213475204444817 / GAUGE**2
LEVEL = 0.7071067811865476
DENSITY = 0.3989422804014327
FACTORS = (1.0, 1.0, DENSITY * GAUGE, 2.0 * DENSITY / GAUGE)


def tall_of(rows):
    return -(-rows // Y)


def first_of(which, rows):
    return jnp.minimum(which * tall_of(rows), rows - tall_of(rows))


def sum_row(theta_ref, m_ref, v_ref, o_ref, out_ref, row):
    days, columns = m_ref.shape[1:]
    for j in range(columns // 128):
        lanes = slice(128 * j, 128 * j + 128)
        a, b, c, d = [
            jnp.broadcast_to(theta_ref[row, f : f + 1, lanes], (8, 128)) for f in range(4)
        ]
        base, slope = jnp.exp(c) * GAUGE**-2, d * d * GAUGE**-2
        sums = None
        for i in range(days // 8):
            at = slice(8 * i, 8 * i + 8)
            m, v, o = m_ref[row, at, lanes], v_ref[row, at, lanes], o_ref[row, at, lanes]
            r = lax.rsqrt(base + slope * v)
            z = ((o - a) - b * m) * r
            q = jnp.exp2((z * z) * POWER)
            k = 1.0 / (1.0 / UNIT + jnp.abs(z))
            tail = TAIL_UNIT[3] - k
            for coefficient in TAIL_UNIT[2::-1]:
                tail = tail * k + coefficient
            g = (tail * k) * q - 1.0
            g = jnp.where(z < 0.0, -g, g)
            h = (q - LEVEL) * r
            terms = [g, g * m, h, h * v]
            sums = terms if sums is None else [s + t for s, t in zip(sums, terms)]
        sums = [jnp.sum(s, axis=0, keepdims=True) for s in sums]
        sums = [sums[0], sums[1], sums[2] * base[:1], sums[3] * d[:1]]
        for f in range(4):
            out_ref[row, f : f + 1, lanes] = sums[f]


def sum_rows(refs, ready=None):
    tall = refs[-1].shape[0]
    turns = tall // GROUP

    def turn(i, carry):
        if ready is not None:
            ready(i * GROUP, GROUP, i)
        for n in range(GROUP):
            sum_row(*refs, i * GROUP + n)
        return carry

    lax.fori_loop(0, turns, turn, 0)
    if tall % GROUP:
        if ready is not None:
            ready(turns * GROUP, tall % GROUP, turns)
        for n in range(turns * GROUP, tall):
            sum_row(*refs, n)


def quarter_copies(at_y, k, sources, targets, sems):
    rows, tall = sources[0].shape[0], targets[0].shape[0]
    first = first_of((at_y[0] + k) % Y, rows)

    def group(start, size, i):
        return [
            pltpu.make_async_copy(
                s.at[pl.ds(first + start, size)], t.at[pl.ds(start, size)], sems.at[i, n]
            )
            for n, (s, t) in enumerate(zip(sources, targets))
        ]

    every = [group(g, min(GROUP, tall - g), g // GROUP) for g in range(0, tall, GROUP)]
    return group, every


def start_all(groups):
    for group in groups:
        for copy in group:
            copy.start()


def wait_all(groups):
    for group in groups:
        for copy in group:
            copy.wait()


def first_kernel(at_y, *refs):
    whole, out_ref, own, ahead = refs[:4], refs[4], refs[5:9], refs[9:13]
    sems, later_sems = refs[13:]
    group, every = quarter_copies(at_y, ORDER[0], whole, own, sems)
    later = quarter_copies(at_y, ORDER[1], whole, ahead, later_sems)[1]
    start_all(every)
    start_all(later)
    sum_rows((own[3], *own[:3], out_ref), lambda *rows: wait_all([group(*rows)]))
    wait_all(later)


def next_kernel(k, at_y, *refs):
    whole, own, out_ref, ahead, sems = refs[:4], refs[4:8], refs[8], refs[9:13], refs[13]
    every = quarter_copies(at_y, k, whole, ahead, sems)[1]
    start_all(every)
    sum_rows((own[3], *own[:3], out_ref))
    wait_all(every)


def last_kernel(*refs):
    sum_rows(refs)


def join_kernel(at_y, *refs):
    pieces, out_ref, sems = refs[:Y], refs[Y], refs[Y + 1]
    rows, tall = out_ref.shape[0], pieces[0].shape[0]
    shorter = rows - (Y - 1) * tall
    for go in (True, False):
        for k in range(Y):
            which = (at_y[0] + k) % Y

            @pl.when(which != Y - 2)
            def _(k=k, which=which):
                at = out_ref.at[pl.ds(first_of(which, rows), tall)]
                copy = pltpu.make_async_copy(pieces[k], at, sems.at[k])
                copy.start() if go else copy.wait()

            @pl.when(which == Y - 2)
            def _(k=k):
                at = out_ref.at[pl.ds((Y - 2) * tall, shorter)]
                copy = pltpu.make_async_copy(pieces[k].at[pl.ds(0, shorter)], at, sems.at[k])
                copy.start() if go else copy.wait()


SMEM = pl.BlockSpec(memory_space=pltpu.SMEM)
VMEM = pl.BlockSpec(memory_space=pltpu.VMEM)
HBM = pl.BlockSpec(memory_space=pltpu.HBM)


def call(kernel, inputs, in_specs, shapes, sems=()):
    size = 1
    for n in shapes[0]:
        size *= n
    cells = size // 4 * 16
    inputs = [
        pltpu.with_memory_space_constraint(x, spec.memory_space) if spec is not SMEM else x
        for x, spec in zip(inputs, in_specs)
    ]
    return pl.pallas_call(
        kernel,
        in_specs=in_specs,
        out_specs=[VMEM] * len(shapes),
        out_shape=[pltpu.VMEM(shape, jnp.float32) for shape in shapes],
        scratch_shapes=[pltpu.SemaphoreType.DMA(s) for s in sems],
        cost_estimate=pl.CostEstimate(flops=40 * cells, transcendentals=3 * cells, bytes_accessed=12 * cells),
        compiler_params=pltpu.CompilerParams(vmem_limit_bytes=4 << 20),
    )(*inputs)


def first_sums(at_y, whole):
    rows, days, columns = whole[0].shape
    tall = tall_of(rows)
    field = (tall, 4, columns)
    quarter = [(tall, days, columns)] * 3 + [field]
    sums, *rest = call(
        first_kernel,
        (at_y, *whole),
        [SMEM] + [HBM] * 4,
        [field] + quarter * 2,
        [(pl.cdiv(tall, GROUP), 4)] * 2,
    )
    own, ahead = rest[:4], rest[4:]
    yield ORDER[0], own[:3], own[3], sums
    for i in (1, 2):
        own = ahead
        sums, *ahead = call(
            functools.partial(next_kernel, ORDER[i + 1]),
            (at_y, *whole, *own),
            [SMEM] + [HBM] * 4 + [VMEM] * 4,
            [field] + quarter,
            [(pl.cdiv(tall, GROUP), 4)],
        )
        yield ORDER[i], own[:3], own[3], sums
    yield ORDER[3], ahead[:3], ahead[3], later_sums(ahead[:3], ahead[3])


def gathered(mine, shifts):
    pieces = {0: mine}
    for k in (2, 1, 3):
        pieces[k] = shift_y(mine, -shifts[k])
    return pieces


def later_steps(data, pieces):
    for k in (0, 2, 1, 3):
        yield k, data[k], pieces[k], later_sums(data[k], pieces[k])


def later_sums(data, theta):
    return call(last_kernel, (theta, *data), [VMEM] * 4, [theta.shape])[0]


def join(at_y, pieces, rows):
    return pl.pallas_call(
        join_kernel,
        in_specs=[SMEM] + [VMEM] * Y,
        out_specs=HBM,
        out_shape=jax.ShapeDtypeStruct((rows, *pieces[0].shape[1:]), jnp.float32),
        scratch_shapes=[pltpu.SemaphoreType.DMA((Y,))],
        compiler_params=pltpu.CompilerParams(vmem_limit_bytes=4 << 20),
        name="join",
    )(at_y, *pieces)


def shift_y(block, by):
    count = lax.axis_size("tm")
    return lax.ppermute(block, "tm", [(i, i // Y * Y + (i + by) % Y) for i in range(count)])


def swap_z(block):
    return lax.ppermute(block, "tm", [(i, i ^ Y) for i in range(lax.axis_size("tm"))])


def halo(flags, pieces):
    send = jnp.where(flags["first"], pieces[3][-2:], pieces[1][:2])
    groups, count = lax.axis_size("tm") // Y, lax.axis_size("space")
    pairs = []
    for g in range(groups):
        for s in range(count):
            over = (g + s // (count - 1)) % groups
            pairs.append(((g * Y) * count + s, over * Y * count + (s + 1) % count))
            pairs.append((((over + 1) * Y - 1) * count + (s + 1) % count, ((g + 1) * Y - 1) * count + s))
    return lax.ppermute(send, ("tm", "space"), pairs)


def laplace(extended):
    middle = extended[1:-1]
    along_lon = extended[2:] + extended[:-2] - 2.0 * middle
    steps = middle[..., 1:] - middle[..., :-1]
    zero = jnp.zeros(middle.shape[:2] + (1,), jnp.float32)
    return along_lon + (
        jnp.concatenate([steps, zero], axis=2) - jnp.concatenate([zero, steps], axis=2)
    )


def smoothed(flags, mine, below, above, edge, rows):
    shared = Y * mine.shape[0] - rows
    tall = mine.shape[0]
    low = jnp.where(flags["last"], below[tall - shared - 2 : tall - shared], below[-2:])
    low = jnp.where(flags["first"], edge, low)
    high = jnp.where(flags["third"], above[shared : shared + 2], above[:2])
    high = jnp.where(flags["last"], edge, high)
    return mine - (STEP * SMOOTH) * laplace(laplace(jnp.concatenate([low, mine, high])))


def on_device(fmean, fvar, obs, theta):
    days, rows, _ = fmean.shape
    scale = jnp.array(FACTORS, jnp.float32).reshape(1, 4, 1) * (STEP / (days * lax.axis_size("tm")))
    y = lax.axis_index("tm") % Y
    at_y = jnp.reshape(y, (1,)).astype(jnp.int32)
    flags = {"first": y == 0, "third": y == Y - 2, "last": y == Y - 1}
    at_y, flags = lax.optimization_barrier((at_y, flags))
    whole = [jnp.transpose(x, (1, 0, 2)) for x in (fmean, fvar, obs, theta)]
    shifts = {1: 1, 2: 2, 3: -1}
    data, pieces = {}, {}
    for step in range(ITERS):
        if step:
            pieces = gathered(mine, shifts)
            made = later_steps(data, pieces)
        else:
            made = first_sums(at_y, whole)
        sums, got = {}, {}
        for k, data[k], pieces[k], sums[k] in made:
            if k:
                got[k] = shift_y(sums[k], shifts[k])
        edge = halo(flags, pieces)
        total = (sums[0] + got[1]) + (got[2] + got[3])
        other = swap_z(total)
        edge = lax.optimization_barrier((edge, total))[0]
        base = smoothed(flags, pieces[0], pieces[3], pieces[1], edge, rows)
        mine = base - scale * (total + other)
    pieces = gathered(mine, shifts)
    return jnp.transpose(join(at_y, [pieces[k] for k in range(Y)], rows), (1, 0, 2))


def solution(mesh):
    days = P("tm", "space", None)
    fields = P(None, "space", None)
    return jax.shard_map(
        on_device,
        mesh=mesh,
        in_specs=(days, days, days, fields),
        out_specs=fields,
        check_vma=False,
    )
```

```python
import functools

import jax
import jax.numpy as jnp
from jax import lax
from jax.experimental import pallas as pl
from jax.experimental.pallas import tpu as pltpu
from jax.sharding import PartitionSpec as P


ITERS = 2
STEP = 0.5
SMOOTH = 0.03
Y = 4
ORDER = (2, 1, 3, 0)
GROUP = 4

BEND = 0.33
TAIL = (
    0.24258075161877687,
    0.4135445348314681,
    -0.19449665181676495,
    0.7602243169976308,
    -0.22185304956855628,
)
UNIT = (-TAIL[4]) ** 0.2
TAIL_UNIT = tuple(c / UNIT ** (i + 1) for i, c in enumerate(TAIL[:4]))
GAUGE = BEND / UNIT
POWER = -0.7213475204444817 / GAUGE**2
LEVEL = 0.7071067811865476
DENSITY = 0.3989422804014327
FACTORS = (1.0, 1.0, DENSITY * GAUGE, 2.0 * DENSITY / GAUGE)


def tall_of(rows):
    return -(-rows // Y)


def first_of(which, rows):
    return jnp.minimum(which * tall_of(rows), rows - tall_of(rows))


def sum_row(theta_ref, m_ref, v_ref, o_ref, out_ref, row):
    days, columns = m_ref.shape[1:]
    for j in range(columns // 128):
        lanes = slice(128 * j, 128 * j + 128)
        a, b, c, d = [
            jnp.broadcast_to(theta_ref[row, f : f + 1, lanes], (8, 128)) for f in range(4)
        ]
        base, slope = jnp.exp(c) * GAUGE**-2, d * d * GAUGE**-2
        sums = None
        for i in range(days // 8):
            at = slice(8 * i, 8 * i + 8)
            m, v, o = m_ref[row, at, lanes], v_ref[row, at, lanes], o_ref[row, at, lanes]
            r = lax.rsqrt(base + slope * v)
            z = ((o - a) - b * m) * r
            q = jnp.exp2((z * z) * POWER)
            k = 1.0 / (1.0 / UNIT + jnp.abs(z))
            tail = TAIL_UNIT[3] - k
            for coefficient in TAIL_UNIT[2::-1]:
                tail = tail * k + coefficient
            g = (tail * k) * q - 1.0
            g = jnp.where(z < 0.0, -g, g)
            h = (q - LEVEL) * r
            terms = [g, g * m, h, h * v]
            sums = terms if sums is None else [s + t for s, t in zip(sums, terms)]
        sums = [jnp.sum(s, axis=0, keepdims=True) for s in sums]
        sums = [sums[0], sums[1], sums[2] * base[:1], sums[3] * d[:1]]
        for f in range(4):
            out_ref[row, f : f + 1, lanes] = sums[f]


def sum_rows(refs, ready=None):
    tall = refs[-1].shape[0]
    turns = tall // GROUP

    def turn(i, carry):
        if ready is not None:
            ready(i * GROUP, GROUP, i)
        for n in range(GROUP):
            sum_row(*refs, i * GROUP + n)
        return carry

    lax.fori_loop(0, turns, turn, 0)
    if tall % GROUP:
        if ready is not None:
            ready(turns * GROUP, tall % GROUP, turns)
        for n in range(turns * GROUP, tall):
            sum_row(*refs, n)


def quarter_copies(at_y, k, sources, targets, sems):
    rows, tall = sources[0].shape[0], targets[0].shape[0]
    first = first_of(at_y[0] ^ k, rows)

    def group(start, size, i):
        return [
            pltpu.make_async_copy(
                s.at[pl.ds(first + start, size)], t.at[pl.ds(start, size)], sems.at[i, n]
            )
            for n, (s, t) in enumerate(zip(sources, targets))
        ]

    every = [group(g, min(GROUP, tall - g), g // GROUP) for g in range(0, tall, GROUP)]
    return group, every


def start_all(groups):
    for group in groups:
        for copy in group:
            copy.start()


def wait_all(groups):
    for group in groups:
        for copy in group:
            copy.wait()


def first_kernel(at_y, *refs):
    whole, out_ref, own, ahead = refs[:4], refs[4], refs[5:9], refs[9:13]
    sems, later_sems = refs[13:]
    group, every = quarter_copies(at_y, ORDER[0], whole, own, sems)
    later = quarter_copies(at_y, ORDER[1], whole, ahead, later_sems)[1]
    start_all(every)
    start_all(later)
    sum_rows((own[3], *own[:3], out_ref), lambda *rows: wait_all([group(*rows)]))
    wait_all(later)


def next_kernel(k, at_y, *refs):
    whole, own, out_ref, ahead, sems = refs[:4], refs[4:8], refs[8], refs[9:13], refs[13]
    every = quarter_copies(at_y, k, whole, ahead, sems)[1]
    start_all(every)
    sum_rows((own[3], *own[:3], out_ref))
    wait_all(every)


def last_kernel(*refs):
    sum_rows(refs)


def join_kernel(at_y, *refs):
    pieces, out_ref, sems = refs[:Y], refs[Y], refs[Y + 1]
    rows, tall = out_ref.shape[0], pieces[0].shape[0]
    shorter = rows - (Y - 1) * tall
    for go in (True, False):
        for k in range(Y):
            which = at_y[0] ^ k

            @pl.when(which != Y - 2)
            def _(k=k, which=which):
                at = out_ref.at[pl.ds(first_of(which, rows), tall)]
                copy = pltpu.make_async_copy(pieces[k], at, sems.at[k])
                copy.start() if go else copy.wait()

            @pl.when(which == Y - 2)
            def _(k=k):
                at = out_ref.at[pl.ds((Y - 2) * tall, shorter)]
                copy = pltpu.make_async_copy(pieces[k].at[pl.ds(0, shorter)], at, sems.at[k])
                copy.start() if go else copy.wait()


SMEM = pl.BlockSpec(memory_space=pltpu.SMEM)
VMEM = pl.BlockSpec(memory_space=pltpu.VMEM)
HBM = pl.BlockSpec(memory_space=pltpu.HBM)


def call(kernel, inputs, in_specs, shapes, sems=()):
    size = 1
    for n in shapes[0]:
        size *= n
    cells = size // 4 * 16
    inputs = [
        pltpu.with_memory_space_constraint(x, spec.memory_space) if spec is not SMEM else x
        for x, spec in zip(inputs, in_specs)
    ]
    return pl.pallas_call(
        kernel,
        in_specs=in_specs,
        out_specs=[VMEM] * len(shapes),
        out_shape=[pltpu.VMEM(shape, jnp.float32) for shape in shapes],
        scratch_shapes=[pltpu.SemaphoreType.DMA(s) for s in sems],
        cost_estimate=pl.CostEstimate(flops=40 * cells, transcendentals=3 * cells, bytes_accessed=12 * cells),
        compiler_params=pltpu.CompilerParams(vmem_limit_bytes=4 << 20),
    )(*inputs)


def first_sums(at_y, whole):
    rows, days, columns = whole[0].shape
    tall = tall_of(rows)
    field = (tall, 4, columns)
    quarter = [(tall, days, columns)] * 3 + [field]
    sums, *rest = call(
        first_kernel,
        (at_y, *whole),
        [SMEM] + [HBM] * 4,
        [field] + quarter * 2,
        [(pl.cdiv(tall, GROUP), 4)] * 2,
    )
    own, ahead = rest[:4], rest[4:]
    yield ORDER[0], own[:3], own[3], sums
    for i in (1, 2):
        own = ahead
        sums, *ahead = call(
            functools.partial(next_kernel, ORDER[i + 1]),
            (at_y, *whole, *own),
            [SMEM] + [HBM] * 4 + [VMEM] * 4,
            [field] + quarter,
            [(pl.cdiv(tall, GROUP), 4)],
        )
        yield ORDER[i], own[:3], own[3], sums
    yield ORDER[3], ahead[:3], ahead[3], later_sums(ahead[:3], ahead[3])


def gathered(mine):
    pieces = {0: mine}
    for k in (2, 1, 3):
        pieces[k] = swap_y(mine, k)
    return pieces


def later_steps(data, pieces):
    for k in (0, 2, 1, 3):
        yield k, data[k], pieces[k], later_sums(data[k], pieces[k])


def later_sums(data, theta):
    return call(last_kernel, (theta, *data), [VMEM] * 4, [theta.shape])[0]


def join(at_y, pieces, rows):
    return pl.pallas_call(
        join_kernel,
        in_specs=[SMEM] + [VMEM] * Y,
        out_specs=HBM,
        out_shape=jax.ShapeDtypeStruct((rows, *pieces[0].shape[1:]), jnp.float32),
        scratch_shapes=[pltpu.SemaphoreType.DMA((Y,))],
        compiler_params=pltpu.CompilerParams(vmem_limit_bytes=4 << 20),
        name="join",
    )(at_y, *pieces)


def swap_y(block, k):
    return lax.ppermute(block, "tm", [(i, i ^ k) for i in range(lax.axis_size("tm"))])


def swap_z(block):
    return lax.ppermute(block, "tm", [(i, i ^ Y) for i in range(lax.axis_size("tm"))])


def halo(flags, across):
    send = jnp.where(flags["first"], across[-2:], across[:2])
    count = lax.axis_size("space")
    pairs = []
    for t in range(lax.axis_size("tm")):
        by = 1 if t % Y < Y // 2 else -1
        pairs += [(t * count + s, t * count + (s + by) % count) for s in range(count)]
    return lax.ppermute(send, ("tm", "space"), pairs)


def laplace(extended):
    middle = extended[1:-1]
    along_lon = extended[2:] + extended[:-2] - 2.0 * middle
    steps = middle[..., 1:] - middle[..., :-1]
    zero = jnp.zeros(middle.shape[:2] + (1,), jnp.float32)
    return along_lon + (
        jnp.concatenate([steps, zero], axis=2) - jnp.concatenate([zero, steps], axis=2)
    )


def smoothed(flags, mine, near, far, edge, rows):
    tall = mine.shape[0]
    shared = Y * tall - rows
    low = jnp.where(flags["odd"], near[-2:], far[-2:])
    low = jnp.where(flags["last"], near[tall - shared - 2 : tall - shared], low)
    low = jnp.where(flags["first"], edge, low)
    high = jnp.where(flags["odd"], far[:2], near[:2])
    high = jnp.where(flags["third"], near[shared : shared + 2], high)
    high = jnp.where(flags["last"], edge, high)
    return mine - (STEP * SMOOTH) * laplace(laplace(jnp.concatenate([low, mine, high])))


def on_device(fmean, fvar, obs, theta):
    days, rows, _ = fmean.shape
    scale = jnp.array(FACTORS, jnp.float32).reshape(1, 4, 1) * (STEP / (days * lax.axis_size("tm")))
    y = lax.axis_index("tm") % Y
    at_y = jnp.reshape(y, (1,)).astype(jnp.int32)
    flags = {"first": y == 0, "odd": y % 2 == 1, "third": y == Y - 2, "last": y == Y - 1}
    at_y, flags = lax.optimization_barrier((at_y, flags))
    whole = [jnp.transpose(x, (1, 0, 2)) for x in (fmean, fvar, obs, theta)]
    data, pieces = {}, {}
    for step in range(ITERS):
        if step:
            pieces = gathered(mine)
            made = later_steps(data, pieces)
        else:
            made = first_sums(at_y, whole)
        sums, got = {}, {}
        for k, data[k], pieces[k], sums[k] in made:
            if k == 2:
                relayed = swap_y(sums[2], 1)
            elif k == 1:
                got[1] = swap_y(sums[1], 1)
            elif k == 3:
                got[3] = swap_y(sums[3] + relayed, 3)
        edge = halo(flags, pieces[3])
        total = (sums[0] + got[1]) + got[3]
        other = swap_z(total)
        edge = lax.optimization_barrier((edge, total))[0]
        base = smoothed(flags, pieces[0], pieces[1], pieces[3], edge, rows)
        mine = base - scale * (total + other)
    pieces = gathered(mine)
    return jnp.transpose(join(at_y, [pieces[k] for k in range(Y)], rows), (1, 0, 2))


def solution(mesh):
    days = P("tm", "space", None)
    fields = P(None, "space", None)
    return jax.shard_map(
        on_device,
        mesh=mesh,
        in_specs=(days, days, days, fields),
        out_specs=fields,
        check_vma=False,
    )
```

```python
import functools

import jax
import jax.numpy as jnp
from jax import lax
from jax.experimental import pallas as pl
from jax.experimental.pallas import tpu as pltpu
from jax.sharding import PartitionSpec as P


ITERS = 2
STEP = 0.5
SMOOTH = 0.03
Y = 4
ORDER = (2, 1, 3, 0)
GROUP = 8

BEND = 0.33
TAIL = (
    0.24258075161877687,
    0.4135445348314681,
    -0.19449665181676495,
    0.7602243169976308,
    -0.22185304956855628,
)
UNIT = (-TAIL[4]) ** 0.2
TAIL_UNIT = tuple(c / UNIT ** (i + 1) for i, c in enumerate(TAIL[:4]))
GAUGE = BEND / UNIT
POWER = -0.7213475204444817 / GAUGE**2
LEVEL = 0.7071067811865476
DENSITY = 0.3989422804014327
FACTORS = (1.0, 1.0, DENSITY * GAUGE, 2.0 * DENSITY / GAUGE)


def tall_of(rows):
    return -(-rows // Y)


def first_of(which, rows):
    return jnp.minimum(which * tall_of(rows), rows - tall_of(rows))


def sum_row(theta_ref, m_ref, v_ref, o_ref, out_ref, row):
    days, columns = m_ref.shape[1:]
    for j in range(columns // 128):
        lanes = slice(128 * j, 128 * j + 128)
        a, b, c, d = [
            jnp.broadcast_to(theta_ref[row, f : f + 1, lanes], (8, 128)) for f in range(4)
        ]
        base, slope = jnp.exp(c) * GAUGE**-2, d * d * GAUGE**-2
        sums = None
        for i in range(days // 8):
            at = slice(8 * i, 8 * i + 8)
            m, v, o = m_ref[row, at, lanes], v_ref[row, at, lanes], o_ref[row, at, lanes]
            r = lax.rsqrt(base + slope * v)
            z = ((o - a) - b * m) * r
            q = jnp.exp2((z * z) * POWER)
            k = 1.0 / (1.0 / UNIT + jnp.abs(z))
            tail = TAIL_UNIT[3] - k
            for coefficient in TAIL_UNIT[2::-1]:
                tail = tail * k + coefficient
            g = (tail * k) * q - 1.0
            g = jnp.where(z < 0.0, -g, g)
            h = (q - LEVEL) * r
            terms = [g, g * m, h, h * v]
            sums = terms if sums is None else [s + t for s, t in zip(sums, terms)]
        sums = [jnp.sum(s, axis=0, keepdims=True) for s in sums]
        sums = [sums[0], sums[1], sums[2] * base[:1], sums[3] * d[:1]]
        for f in range(4):
            out_ref[row, f : f + 1, lanes] = sums[f]


def sum_rows(refs, ready=None):
    tall = refs[-1].shape[0]
    turns = tall // GROUP

    def turn(i, carry):
        if ready is not None:
            ready(i * GROUP, GROUP, i)
        for n in range(GROUP):
            sum_row(*refs, i * GROUP + n)
        return carry

    lax.fori_loop(0, turns, turn, 0)
    if tall % GROUP:
        if ready is not None:
            ready(turns * GROUP, tall % GROUP, turns)
        for n in range(turns * GROUP, tall):
            sum_row(*refs, n)


def quarter_copies(at_y, k, sources, targets, sems):
    rows, tall = sources[0].shape[0], targets[0].shape[0]
    first = first_of(at_y[0] ^ k, rows)

    def group(start, size, i):
        return [
            pltpu.make_async_copy(
                s.at[pl.ds(first + start, size)], t.at[pl.ds(start, size)], sems.at[i, n]
            )
            for n, (s, t) in enumerate(zip(sources, targets))
        ]

    every = [group(g, min(GROUP, tall - g), g // GROUP) for g in range(0, tall, GROUP)]
    return group, every


def start_all(groups):
    for group in groups:
        for copy in group:
            copy.start()


def wait_all(groups):
    for group in groups:
        for copy in group:
            copy.wait()


def first_kernel(at_y, *refs):
    whole, out_ref, own, ahead = refs[:4], refs[4], refs[5:9], refs[9:13]
    sems, later_sems = refs[13:]
    group, every = quarter_copies(at_y, ORDER[0], whole, own, sems)
    later = quarter_copies(at_y, ORDER[1], whole, ahead, later_sems)[1]
    start_all(every)
    start_all(later)
    sum_rows((own[3], *own[:3], out_ref), lambda *rows: wait_all([group(*rows)]))
    wait_all(later)


def next_kernel(k, at_y, *refs):
    whole, own, out_ref, ahead, sems = refs[:4], refs[4:8], refs[8], refs[9:13], refs[13]
    every = quarter_copies(at_y, k, whole, ahead, sems)[1]
    start_all(every)
    sum_rows((own[3], *own[:3], out_ref))
    wait_all(every)


def last_kernel(*refs):
    sum_rows(refs)


def join_kernel(at_y, *refs):
    pieces, out_ref, sems = refs[:Y], refs[Y], refs[Y + 1]
    rows, tall = out_ref.shape[0], pieces[0].shape[0]
    shorter = rows - (Y - 1) * tall
    for go in (True, False):
        for k in range(Y):
            which = at_y[0] ^ k

            @pl.when(which != Y - 2)
            def _(k=k, which=which):
                at = out_ref.at[pl.ds(first_of(which, rows), tall)]
                copy = pltpu.make_async_copy(pieces[k], at, sems.at[k])
                copy.start() if go else copy.wait()

            @pl.when(which == Y - 2)
            def _(k=k):
                at = out_ref.at[pl.ds((Y - 2) * tall, shorter)]
                copy = pltpu.make_async_copy(pieces[k].at[pl.ds(0, shorter)], at, sems.at[k])
                copy.start() if go else copy.wait()


SMEM = pl.BlockSpec(memory_space=pltpu.SMEM)
VMEM = pl.BlockSpec(memory_space=pltpu.VMEM)
HBM = pl.BlockSpec(memory_space=pltpu.HBM)


def call(kernel, inputs, in_specs, shapes, sems=()):
    size = 1
    for n in shapes[0]:
        size *= n
    cells = size // 4 * 16
    inputs = [
        pltpu.with_memory_space_constraint(x, spec.memory_space) if spec is not SMEM else x
        for x, spec in zip(inputs, in_specs)
    ]
    return pl.pallas_call(
        kernel,
        in_specs=in_specs,
        out_specs=[VMEM] * len(shapes),
        out_shape=[pltpu.VMEM(shape, jnp.float32) for shape in shapes],
        scratch_shapes=[pltpu.SemaphoreType.DMA(s) for s in sems],
        cost_estimate=pl.CostEstimate(flops=40 * cells, transcendentals=3 * cells, bytes_accessed=12 * cells),
        compiler_params=pltpu.CompilerParams(vmem_limit_bytes=4 << 20),
    )(*inputs)


def first_sums(at_y, whole):
    rows, days, columns = whole[0].shape
    tall = tall_of(rows)
    field = (tall, 4, columns)
    quarter = [(tall, days, columns)] * 3 + [field]
    sums, *rest = call(
        first_kernel,
        (at_y, *whole),
        [SMEM] + [HBM] * 4,
        [field] + quarter * 2,
        [(pl.cdiv(tall, GROUP), 4)] * 2,
    )
    own, ahead = rest[:4], rest[4:]
    yield ORDER[0], own[:3], own[3], sums
    for i in (1, 2):
        own = ahead
        sums, *ahead = call(
            functools.partial(next_kernel, ORDER[i + 1]),
            (at_y, *whole, *own),
            [SMEM] + [HBM] * 4 + [VMEM] * 4,
            [field] + quarter,
            [(pl.cdiv(tall, GROUP), 4)],
        )
        yield ORDER[i], own[:3], own[3], sums
    yield ORDER[3], ahead[:3], ahead[3], later_sums(ahead[:3], ahead[3])


def gathered(mine):
    pieces = {0: mine}
    for k in (2, 1, 3):
        pieces[k] = swap_y(mine, k)
    return pieces


def later_steps(data, pieces):
    for k in (0, 1, 3, 2):
        yield k, data[k], pieces[k], later_sums(data[k], pieces[k])


def later_sums(data, theta):
    return call(last_kernel, (theta, *data), [VMEM] * 4, [theta.shape])[0]


def join(at_y, pieces, rows):
    return pl.pallas_call(
        join_kernel,
        in_specs=[SMEM] + [VMEM] * Y,
        out_specs=HBM,
        out_shape=jax.ShapeDtypeStruct((rows, *pieces[0].shape[1:]), jnp.float32),
        scratch_shapes=[pltpu.SemaphoreType.DMA((Y,))],
        compiler_params=pltpu.CompilerParams(vmem_limit_bytes=4 << 20),
        name="join",
    )(at_y, *pieces)


def swap_y(block, k):
    return lax.ppermute(block, "tm", [(i, i ^ k) for i in range(lax.axis_size("tm"))])


def swap_z(block):
    return lax.ppermute(block, "tm", [(i, i ^ Y) for i in range(lax.axis_size("tm"))])


def halo(flags, across):
    send = jnp.where(flags["first"], across[-2:], across[:2])
    count = lax.axis_size("space")
    pairs = []
    for t in range(lax.axis_size("tm")):
        by = 1 if t % Y < Y // 2 else -1
        pairs += [(t * count + s, t * count + (s + by) % count) for s in range(count)]
    return lax.ppermute(send, ("tm", "space"), pairs)


def laplace(extended):
    middle = extended[1:-1]
    along_lon = extended[2:] + extended[:-2] - 2.0 * middle
    steps = middle[..., 1:] - middle[..., :-1]
    zero = jnp.zeros(middle.shape[:2] + (1,), jnp.float32)
    return along_lon + (
        jnp.concatenate([steps, zero], axis=2) - jnp.concatenate([zero, steps], axis=2)
    )


def smoothed(flags, mine, near, far, edge, rows):
    tall = mine.shape[0]
    shared = Y * tall - rows
    low = jnp.where(flags["odd"], near[-2:], far[-2:])
    low = jnp.where(flags["last"], near[tall - shared - 2 : tall - shared], low)
    low = jnp.where(flags["first"], edge, low)
    high = jnp.where(flags["odd"], far[:2], near[:2])
    high = jnp.where(flags["third"], near[shared : shared + 2], high)
    high = jnp.where(flags["last"], edge, high)
    return mine - (STEP * SMOOTH) * laplace(laplace(jnp.concatenate([low, mine, high])))


def on_device(fmean, fvar, obs, theta):
    days, rows, _ = fmean.shape
    scale = jnp.array(FACTORS, jnp.float32).reshape(1, 4, 1) * (STEP / (days * lax.axis_size("tm")))
    y = lax.axis_index("tm") % Y
    at_y = jnp.reshape(y, (1,)).astype(jnp.int32)
    flags = {"first": y == 0, "odd": y % 2 == 1, "third": y == Y - 2, "last": y == Y - 1}
    at_y, flags = lax.optimization_barrier((at_y, flags))
    whole = [jnp.transpose(x, (1, 0, 2)) for x in (fmean, fvar, obs, theta)]
    data, pieces = {}, {}
    for step in range(ITERS):
        if step:
            pieces = gathered(mine)
            made = later_steps(data, pieces)
        else:
            made = first_sums(at_y, whole)
        sums, got = {}, {}
        for k, data[k], pieces[k], sums[k] in made:
            if k == 2 and step == 0:
                relayed = swap_y(sums[2], 1)
            elif k:
                out = sums[k] + relayed if k == 3 and step == 0 else sums[k]
                got[k] = swap_y(out, k)
        edge = halo(flags, pieces[3])
        total = (sums[0] + got[1]) + got[3]
        if step:
            total = total + got[2]
        other = swap_z(total)
        edge = lax.optimization_barrier((edge, total))[0]
        base = smoothed(flags, pieces[0], pieces[1], pieces[3], edge, rows)
        mine = base - scale * (total + other)
    pieces = gathered(mine)
    return jnp.transpose(join(at_y, [pieces[k] for k in range(Y)], rows), (1, 0, 2))


def solution(mesh):
    days = P("tm", "space", None)
    fields = P(None, "space", None)
    return jax.shard_map(
        on_device,
        mesh=mesh,
        in_specs=(days, days, days, fields),
        out_specs=fields,
        check_vma=False,
    )
```

```python
import functools

import jax
import jax.numpy as jnp
from jax import lax
from jax.experimental import pallas as pl
from jax.experimental.pallas import tpu as pltpu
from jax.sharding import PartitionSpec as P


ITERS = 2
STEP = 0.5
SMOOTH = 0.03
Y = 4
ORDER = (2, 1, 3, 0)
GROUP = 8
LOOP = 12

BEND = 0.33
TAIL = (
    0.24258075161877687,
    0.4135445348314681,
    -0.19449665181676495,
    0.7602243169976308,
    -0.22185304956855628,
)
UNIT = (-TAIL[4]) ** 0.2
TAIL_UNIT = tuple(c / UNIT ** (i + 1) for i, c in enumerate(TAIL[:4]))
GAUGE = BEND / UNIT
POWER = -0.7213475204444817 / GAUGE**2
LEVEL = 0.7071067811865476
DENSITY = 0.3989422804014327
FACTORS = (1.0, 1.0, DENSITY * GAUGE, 2.0 * DENSITY / GAUGE)


def tall_of(rows):
    return -(-rows // Y)


def first_of(which, rows):
    return jnp.minimum(which * tall_of(rows), rows - tall_of(rows))


def sum_row(theta_ref, m_ref, v_ref, o_ref, out_ref, row):
    days, columns = m_ref.shape[1:]
    for j in range(columns // 128):
        lanes = slice(128 * j, 128 * j + 128)
        a, b, c, d = [
            jnp.broadcast_to(theta_ref[row, f : f + 1, lanes], (8, 128)) for f in range(4)
        ]
        base, slope = jnp.exp(c) * GAUGE**-2, d * d * GAUGE**-2
        sums = None
        for i in range(days // 8):
            at = slice(8 * i, 8 * i + 8)
            m, v, o = m_ref[row, at, lanes], v_ref[row, at, lanes], o_ref[row, at, lanes]
            r = lax.rsqrt(base + slope * v)
            z = ((o - a) - b * m) * r
            q = jnp.exp2((z * z) * POWER)
            k = 1.0 / (1.0 / UNIT + jnp.abs(z))
            tail = TAIL_UNIT[3] - k
            for coefficient in TAIL_UNIT[2::-1]:
                tail = tail * k + coefficient
            g = (tail * k) * q - 1.0
            g = jnp.where(z < 0.0, -g, g)
            h = (q - LEVEL) * r
            terms = [g, g * m, h, h * v]
            sums = terms if sums is None else [s + t for s, t in zip(sums, terms)]
        sums = [jnp.sum(s, axis=0, keepdims=True) for s in sums]
        sums = [sums[0], sums[1], sums[2] * base[:1], sums[3] * d[:1]]
        for f in range(4):
            out_ref[row, f : f + 1, lanes] = sums[f]


def sum_rows(refs, ready=None):
    tall = refs[-1].shape[0]
    size = LOOP if ready is None else GROUP
    turns = tall // size

    def turn(i, carry):
        if ready is not None:
            ready(i * size, size, i)
        for n in range(size):
            sum_row(*refs, i * size + n)
        return carry

    lax.fori_loop(0, turns, turn, 0)
    if tall % size:
        if ready is not None:
            ready(turns * size, tall % size, turns)
        for n in range(turns * size, tall):
            sum_row(*refs, n)


def quarter_copies(at_y, k, sources, targets, sems):
    rows, tall = sources[0].shape[0], targets[0].shape[0]
    first = first_of(at_y[0] ^ k, rows)

    def group(start, size, i):
        return [
            pltpu.make_async_copy(
                s.at[pl.ds(first + start, size)], t.at[pl.ds(start, size)], sems.at[i, n]
            )
            for n, (s, t) in enumerate(zip(sources, targets))
        ]

    every = [group(g, min(GROUP, tall - g), g // GROUP) for g in range(0, tall, GROUP)]
    return group, every


def start_all(groups):
    for group in groups:
        for copy in group:
            copy.start()


def wait_all(groups):
    for group in groups:
        for copy in group:
            copy.wait()


def first_kernel(at_y, *refs):
    whole, out_ref, own, ahead = refs[:4], refs[4], refs[5:9], refs[9:13]
    sems, later_sems = refs[13:]
    group, every = quarter_copies(at_y, ORDER[0], whole, own, sems)
    later = quarter_copies(at_y, ORDER[1], whole, ahead, later_sems)[1]
    start_all(every)
    start_all(later)
    sum_rows((own[3], *own[:3], out_ref), lambda *rows: wait_all([group(*rows)]))
    wait_all(later)


def next_kernel(k, at_y, *refs):
    whole, own, out_ref, ahead, sems = refs[:4], refs[4:8], refs[8], refs[9:13], refs[13]
    every = quarter_copies(at_y, k, whole, ahead, sems)[1]
    start_all(every)
    sum_rows((own[3], *own[:3], out_ref))
    wait_all(every)


def last_kernel(*refs):
    sum_rows(refs)


def join_kernel(at_y, *refs):
    pieces, out_ref, sems = refs[:Y], refs[Y], refs[Y + 1]
    rows, tall = out_ref.shape[0], pieces[0].shape[0]
    shorter = rows - (Y - 1) * tall
    for go in (True, False):
        for k in range(Y):
            which = at_y[0] ^ k

            @pl.when(which != Y - 2)
            def _(k=k, which=which):
                at = out_ref.at[pl.ds(first_of(which, rows), tall)]
                copy = pltpu.make_async_copy(pieces[k], at, sems.at[k])
                copy.start() if go else copy.wait()

            @pl.when(which == Y - 2)
            def _(k=k):
                at = out_ref.at[pl.ds((Y - 2) * tall, shorter)]
                copy = pltpu.make_async_copy(pieces[k].at[pl.ds(0, shorter)], at, sems.at[k])
                copy.start() if go else copy.wait()


SMEM = pl.BlockSpec(memory_space=pltpu.SMEM)
VMEM = pl.BlockSpec(memory_space=pltpu.VMEM)
HBM = pl.BlockSpec(memory_space=pltpu.HBM)


def call(kernel, inputs, in_specs, shapes, sems=()):
    size = 1
    for n in shapes[0]:
        size *= n
    cells = size // 4 * 16
    inputs = [
        pltpu.with_memory_space_constraint(x, spec.memory_space) if spec is not SMEM else x
        for x, spec in zip(inputs, in_specs)
    ]
    return pl.pallas_call(
        kernel,
        in_specs=in_specs,
        out_specs=[VMEM] * len(shapes),
        out_shape=[pltpu.VMEM(shape, jnp.float32) for shape in shapes],
        scratch_shapes=[pltpu.SemaphoreType.DMA(s) for s in sems],
        cost_estimate=pl.CostEstimate(flops=40 * cells, transcendentals=3 * cells, bytes_accessed=12 * cells),
        compiler_params=pltpu.CompilerParams(vmem_limit_bytes=4 << 20),
    )(*inputs)


def first_sums(at_y, whole):
    rows, days, columns = whole[0].shape
    tall = tall_of(rows)
    field = (tall, 4, columns)
    quarter = [(tall, days, columns)] * 3 + [field]
    sums, *rest = call(
        first_kernel,
        (at_y, *whole),
        [SMEM] + [HBM] * 4,
        [field] + quarter * 2,
        [(pl.cdiv(tall, GROUP), 4)] * 2,
    )
    own, ahead = rest[:4], rest[4:]
    yield ORDER[0], own[:3], own[3], sums
    for i in (1, 2):
        own = ahead
        sums, *ahead = call(
            functools.partial(next_kernel, ORDER[i + 1]),
            (at_y, *whole, *own),
            [SMEM] + [HBM] * 4 + [VMEM] * 4,
            [field] + quarter,
            [(pl.cdiv(tall, GROUP), 4)],
        )
        yield ORDER[i], own[:3], own[3], sums
    yield ORDER[3], ahead[:3], ahead[3], later_sums(ahead[:3], ahead[3])


def gathered(mine):
    pieces = {0: mine}
    for k in (2, 1, 3):
        pieces[k] = swap_y(mine, k)
    return pieces


def later_steps(data, pieces):
    for k in (0, 1, 3, 2):
        yield k, data[k], pieces[k], later_sums(data[k], pieces[k])


def later_sums(data, theta):
    return call(last_kernel, (theta, *data), [VMEM] * 4, [theta.shape])[0]


def join(at_y, pieces, rows):
    return pl.pallas_call(
        join_kernel,
        in_specs=[SMEM] + [VMEM] * Y,
        out_specs=HBM,
        out_shape=jax.ShapeDtypeStruct((rows, *pieces[0].shape[1:]), jnp.float32),
        scratch_shapes=[pltpu.SemaphoreType.DMA((Y,))],
        compiler_params=pltpu.CompilerParams(vmem_limit_bytes=4 << 20),
        name="join",
    )(at_y, *pieces)


def swap_y(block, k):
    return lax.ppermute(block, "tm", [(i, i ^ k) for i in range(lax.axis_size("tm"))])


def swap_z(block):
    return lax.ppermute(block, "tm", [(i, i ^ Y) for i in range(lax.axis_size("tm"))])


def halo(flags, across):
    send = jnp.where(flags["first"], across[-2:], across[:2])
    count = lax.axis_size("space")
    pairs = []
    for t in range(lax.axis_size("tm")):
        by = 1 if t % Y < Y // 2 else -1
        pairs += [(t * count + s, t * count + (s + by) % count) for s in range(count)]
    return lax.ppermute(send, ("tm", "space"), pairs)


def laplace(extended):
    middle = extended[1:-1]
    along_lon = extended[2:] + extended[:-2] - 2.0 * middle
    steps = middle[..., 1:] - middle[..., :-1]
    zero = jnp.zeros(middle.shape[:2] + (1,), jnp.float32)
    return along_lon + (
        jnp.concatenate([steps, zero], axis=2) - jnp.concatenate([zero, steps], axis=2)
    )


def smoothed(flags, mine, near, far, edge, rows):
    tall = mine.shape[0]
    shared = Y * tall - rows
    low = jnp.where(flags["odd"], near[-2:], far[-2:])
    low = jnp.where(flags["last"], near[tall - shared - 2 : tall - shared], low)
    low = jnp.where(flags["first"], edge, low)
    high = jnp.where(flags["odd"], far[:2], near[:2])
    high = jnp.where(flags["third"], near[shared : shared + 2], high)
    high = jnp.where(flags["last"], edge, high)
    return mine - (STEP * SMOOTH) * laplace(laplace(jnp.concatenate([low, mine, high])))


def on_device(fmean, fvar, obs, theta):
    days, rows, _ = fmean.shape
    scale = jnp.array(FACTORS, jnp.float32).reshape(1, 4, 1) * (STEP / (days * lax.axis_size("tm")))
    y = lax.axis_index("tm") % Y
    at_y = jnp.reshape(y, (1,)).astype(jnp.int32)
    flags = {"first": y == 0, "odd": y % 2 == 1, "third": y == Y - 2, "last": y == Y - 1}
    at_y, flags = lax.optimization_barrier((at_y, flags))
    whole = [jnp.transpose(x, (1, 0, 2)) for x in (fmean, fvar, obs, theta)]
    data, pieces = {}, {}
    for step in range(ITERS):
        if step:
            pieces = gathered(mine)
            made = later_steps(data, pieces)
        else:
            made = first_sums(at_y, whole)
        sums, got = {}, {}
        for k, data[k], pieces[k], sums[k] in made:
            if k == 2 and step == 0:
                relayed = swap_y(sums[2], 1)
            elif k:
                out = sums[k] + relayed if k == 3 and step == 0 else sums[k]
                got[k] = swap_y(out, k)
        edge = halo(flags, pieces[3])
        total = (sums[0] + got[1]) + got[3]
        if step:
            total = total + got[2]
        other = swap_z(total)
        edge = lax.optimization_barrier((edge, total))[0]
        base = smoothed(flags, pieces[0], pieces[1], pieces[3], edge, rows)
        mine = base - scale * (total + other)
    pieces = gathered(mine)
    return jnp.transpose(join(at_y, [pieces[k] for k in range(Y)], rows), (1, 0, 2))


def solution(mesh):
    days = P("tm", "space", None)
    fields = P(None, "space", None)
    return jax.shard_map(
        on_device,
        mesh=mesh,
        in_specs=(days, days, days, fields),
        out_specs=fields,
        check_vma=False,
    )
```
